32 devices in a mesh: pipe: 4 (over x, core), rep: 8 (over z, y).
Axes of the slice: x: 2, y: 2, z: 4, core: 2. Of those that a mesh axis runs over, the one named last changes fastest.
Arguments:
- activations: bfloat16 [4, 8, 1, 8, 32, 384], P('pipe', 'rep'), may hold values from -8 to 8, as said below
- preactivation: bfloat16 [4, 8, 1, 8, 32, 384], P('pipe', 'rep'), may hold values from -6 to 6
- upstream: bfloat16 [4, 8, 1, 8, 32, 384], P('pipe', 'rep'), may hold values from -12 to 12, as said below
- weights: bfloat16 [4, 3456, 384], P('pipe'), may hold values from -0.109375 to 0.109375
- master: float32 [4, 8, 165888], P('pipe', 'rep'), may hold values from -0.3125 to 0.3125
- momentum: float32 [4, 8, 165888], P('pipe', 'rep'), may hold values from -6 to 6
Outputs:
- passed_grad: bfloat16 [4, 8, 1, 8, 32, 384], P('pipe', 'rep')
- new_momentum: float32 [4, 8, 165888], P('pipe', 'rep')
- new_weights: float32 [4, 8, 165888], P('pipe', 'rep')
The draws below stay inside these ranges and needn't reach their ends.
Inputs may be any that keep to these rules, and one draw needn't show every extreme that they name: `activations`: Normal-like values; replicas of one section share part of their values. `upstream`: Normal-like values with a scale that differs from replica to replica; replicas of one section share part of their values.
All inputs are finite; a program needn't handle non-finite values.
Results may differ from the reference program's by a relative error of at most 0.0057.
Values may be sent and summed in bfloat16 or wider, within the bound.
A program may use at most 64 MiB of HBM per device.

```python
import jax
import jax.numpy as jnp
from jax import lax

C = 384
KTAPS = 9
HROWS = 8
WCOLS = 32
FRAMES = 1
PARAMS = 1327104
BLOCK = 165888
N_PIPE = 4
N_REP = 8


def draw_activations(key, part):
    full_shape = (N_PIPE, N_REP, FRAMES, HROWS, WCOLS, C)
    common = jax.random.normal(jax.random.fold_in(key, 101), (N_PIPE, 1, FRAMES, HROWS, WCOLS, C), jnp.float32)
    noise = jax.random.normal(jax.random.fold_in(key, 202), full_shape, jnp.float32)
    band = jnp.arange(C) * 16 // C
    shared_band = ((band < 8) & (band % 2 == 0)).astype(jnp.float32)
    common_weight = 0.15 + shared_band * (1.94 - 0.15)
    noise_weight = 0.989 + shared_band * (0.486 - 0.989)
    blended = common_weight * common + noise_weight * noise
    return jnp.clip(blended, -8.0, 8.0).astype(jnp.bfloat16)


def draw_upstream(key, part):
    full_shape = (N_PIPE, N_REP, FRAMES, HROWS, WCOLS, C)
    common = jax.random.normal(jax.random.fold_in(key, 404), (N_PIPE, 1, FRAMES, HROWS, WCOLS, C), jnp.float32)
    noise = jax.random.normal(jax.random.fold_in(key, 505), full_shape, jnp.float32)
    ramp = jnp.arange(N_REP).astype(jnp.float32) / max(N_REP - 1, 1)
    jitter = jax.random.uniform(jax.random.fold_in(key, 606), (N_PIPE, N_REP), jnp.float32, 0.8, 1.25)
    replica_scale = (jnp.exp(jnp.log(3.0) * ramp)[None, :] * jitter).reshape(N_PIPE, N_REP, 1, 1, 1, 1)
    blended = replica_scale * (0.85 * common + 0.5 * noise)
    return jnp.clip(blended, -12.0, 12.0).astype(jnp.bfloat16)


def level_of(own_key, shape, cuts, smallest, top_value):
    loudness, own = 1.0, jax.random.fold_in(own_key, 6)
    for dim, blocks in cuts:
        heights = jnp.exp(jax.random.uniform(jax.random.fold_in(own, dim), (blocks,), jnp.float32, smallest / len(cuts), top_value / len(cuts)))
        loudness = loudness * jnp.repeat(heights, shape[dim] // blocks).reshape([-1 if axis == dim else 1 for axis in range(len(shape))])
    return loudness


def centred(stream_key, shape, deviation, reach, cuts=(), dtype=jnp.bfloat16):
    entries = deviation * jax.random.normal(stream_key, shape, jnp.float32)
    if cuts:
        entries = entries * level_of(stream_key, shape, cuts, -0.22, 0.18)
    return jnp.clip(entries, -reach, reach).astype(dtype)


def setup_inputs(seed: int = 0) -> dict:
    streams_of = jax.random.split(jax.random.key(seed), 7)
    activations = draw_activations(jax.random.fold_in(streams_of[6], 71), 0)
    preactivation = centred(streams_of[1], (N_PIPE, N_REP, FRAMES, HROWS, WCOLS, C), 1.5, 6.0, ((0, 4), (1, 8)))
    upstream = draw_upstream(jax.random.fold_in(streams_of[6], 71), 0)
    weights = centred(streams_of[3], (N_PIPE, KTAPS * C, C), (KTAPS * C) ** -0.5, 0.109375, ((0, 4),))
    master = centred(streams_of[4], (N_PIPE, N_REP, BLOCK), C ** -0.5, 0.3125, ((0, 4), (1, 8)), jnp.float32)
    momentum = centred(streams_of[5], (N_PIPE, N_REP, BLOCK), 1.0, 6.0, ((0, 4), (1, 8)), jnp.float32)
    return {"activations": activations, "preactivation": preactivation, "upstream": upstream, "weights": weights, "master": master, "momentum": momentum}


EPS = 1e-6


def tile_patches(tile_data):
    frames, tile_rows, tile_cols, channels = tile_data.shape
    padded = jnp.pad(tile_data, ((0, 0), (1, 1), (1, 1), (0, 0)))
    pieces = [padded[:, row_off:row_off + tile_rows, col_off:col_off + tile_cols, :] for row_off in range(3) for col_off in range(3)]
    return jnp.concatenate(pieces, axis=-1).reshape(frames * tile_rows * tile_cols, 9 * channels)


def local_backward(tile_data, preact_tile, upstream_tile, kernel):
    frames, tile_rows, tile_cols, channels = tile_data.shape
    pre_float = preact_tile.astype(jnp.float32)
    sigmoid_val = jax.nn.sigmoid(pre_float)
    local_grad = (upstream_tile.astype(jnp.float32) * sigmoid_val * (1.0 + pre_float * (1.0 - sigmoid_val))).astype(jnp.bfloat16)
    flat_grad = local_grad.reshape(-1, channels)
    patches = tile_patches(tile_data)
    weight_grad = lax.dot_general(patches, flat_grad, (((0,), (0,)), ((), ())), preferred_element_type=jnp.float32).astype(jnp.bfloat16)
    spread = lax.dot_general(flat_grad, kernel, (((1,), (1,)), ((), ())), preferred_element_type=jnp.float32)
    spread = spread.reshape(frames, tile_rows, tile_cols, 9, channels)
    padded = jnp.pad(spread, ((0, 0), (1, 1), (1, 1), (0, 0), (0, 0)))
    summed = jnp.zeros((frames, tile_rows, tile_cols, channels), jnp.float32)
    for row_off in range(3):
        for col_off in range(3):
            summed = summed + padded[:, 2 - row_off:2 - row_off + tile_rows, 2 - col_off:2 - col_off + tile_cols, row_off * 3 + col_off, :]
    return weight_grad, summed.astype(jnp.bfloat16)


def adasum_pair(pair_rows):
    lower = pair_rows[0].astype(jnp.float32)
    upper = pair_rows[1].astype(jnp.float32)
    cross = jnp.sum(lower * upper)
    lower_sq = jnp.sum(lower * lower)
    upper_sq = jnp.sum(upper * upper)
    merged = (1.0 - cross / (2.0 * lower_sq + EPS)) * lower + (1.0 - cross / (2.0 * upper_sq + EPS)) * upper
    return merged.astype(jnp.bfloat16)


def section_step(inputs):
    tile_data, preact_tile, upstream_tile, kernel, master_shards, momentum_shards = inputs

    def replica_step(replica_inputs):
        return local_backward(replica_inputs[0], replica_inputs[1], replica_inputs[2], kernel)

    weight_grads, input_grads = lax.map(replica_step, (tile_data, preact_tile, upstream_tile))
    vectors = weight_grads.reshape(N_REP, PARAMS)
    remaining = N_REP
    while remaining > 1:
        vectors = lax.map(adasum_pair, vectors.reshape(remaining // 2, 2, PARAMS))
        remaining = remaining // 2
    combined = vectors.reshape(N_REP, BLOCK).astype(jnp.float32)
    updated_momentum = 0.9 * momentum_shards + 0.0625 * combined
    updated_weights = master_shards - 0.02 * updated_momentum
    return input_grads, updated_momentum, updated_weights


def reference(activations, preactivation, upstream, weights, master, momentum):
    input_grads, new_momentum, new_weights = lax.map(section_step, (activations, preactivation, upstream, weights, master, momentum))
    passed_grad = jnp.concatenate([input_grads[1:], jnp.zeros_like(input_grads[:1])], axis=0)
    return passed_grad, new_momentum, new_weights
```

```python
import functools

import jax
import jax.numpy as jnp
from jax import lax
from jax.experimental import pallas as pl
from jax.experimental.pallas import tpu as pltpu
from jax.sharding import PartitionSpec as P

EPS = 1e-06


def swapped(shard, axis, stride):
    return lax.ppermute(shard, axis, [(i, i ^ 1 << stride) for i in range(lax.axis_size(axis))])


def from_behind(shard, axis, by):
    count = lax.axis_size(axis)
    pairs = [(i, i + by) for i in range(count) if 0 <= i + by < count]
    return lax.ppermute(shard, axis, pairs)


def shifted_patches(tile_data, flipped):
    frames, tile_rows, tile_cols, channels = tile_data.shape
    padded = jnp.pad(tile_data, ((0, 0), (1, 1), (1, 1), (0, 0)))
    if flipped:
        offsets = [(2 - row_off, 2 - col_off) for row_off in range(3) for col_off in range(3)]
    else:
        offsets = [(row_off, col_off) for row_off in range(3) for col_off in range(3)]
    pieces = [
        padded[:, first : first + tile_rows, second : second + tile_cols, :]
        for first, second in offsets
    ]
    return jnp.concatenate(pieces, axis=-1).reshape(frames * tile_rows * tile_cols, 9 * channels)


def local_backward(tile_data, preact_tile, upstream_tile, kernel):
    frames, tile_rows, tile_cols, channels = tile_data.shape
    pre_float = preact_tile.astype(jnp.float32)
    sigmoid_val = jax.nn.sigmoid(pre_float)
    local_grad = (
        upstream_tile.astype(jnp.float32) * sigmoid_val * (1.0 + pre_float * (1.0 - sigmoid_val))
    ).astype(jnp.bfloat16)
    flat_grad = local_grad.reshape(-1, channels)
    patches = shifted_patches(tile_data, False)
    weight_grad = lax.dot_general(
        patches, flat_grad, (((0,), (0,)), ((), ())), preferred_element_type=jnp.float32
    ).astype(jnp.bfloat16)
    grad_patches = shifted_patches(local_grad, True).reshape(-1, 9, channels)
    kernel_taps = kernel.reshape(9, channels, channels)
    summed = lax.dot_general(
        grad_patches, kernel_taps, (((1, 2), (0, 2)), ((), ())), preferred_element_type=jnp.float32
    )
    return (
        weight_grad,
        summed.astype(jnp.bfloat16).reshape(frames, tile_rows, tile_cols, channels),
    )


def group_sum(partials, sum_bits):
    for bit_number in range(sum_bits):
        partials = partials + swapped(partials, "rep", bit_number)
    return partials


def body(activations, preactivation, upstream, weights, master, momentum):
    weight_grad, input_grad = local_backward(
        activations[0, 0], preactivation[0, 0], upstream[0, 0], weights[0]
    )
    passed = from_behind(input_grad, "pipe", -1)
    replicas = lax.axis_size("rep")
    level_count = replicas.bit_length() - 1
    rep_index = lax.axis_index("rep")
    held_rows = weight_grad.reshape(replicas, -1)
    for level_num in range(level_count):
        is_lower = jnp.right_shift(rep_index, level_num) & 1 == 0
        paired = held_rows.reshape(-1, 2, held_rows.shape[1])
        keep_rows = jnp.where(is_lower, paired[:, 0], paired[:, 1])
        give_rows = jnp.where(is_lower, paired[:, 1], paired[:, 0])
        other_rows = swapped(give_rows, "rep", level_num)
        keep_float = keep_rows.astype(jnp.float32)
        other_float = other_rows.astype(jnp.float32)
        keep_sq = jnp.sum(keep_float * keep_float)
        other_sq = jnp.sum(other_float * other_float)
        partials = jnp.stack(
            [
                jnp.where(is_lower, keep_sq, other_sq),
                jnp.where(is_lower, other_sq, keep_sq),
                jnp.sum(keep_float * other_float),
            ]
        )
        sum_bits = level_num + 1
        partials = group_sum(partials, sum_bits)
        lower_coef = 1.0 - partials[2] / (2.0 * partials[0] + EPS)
        upper_coef = 1.0 - partials[2] / (2.0 * partials[1] + EPS)
        keep_coef = jnp.where(is_lower, lower_coef, upper_coef)
        other_coef = jnp.where(is_lower, upper_coef, lower_coef)
        merged = keep_coef * keep_rows.astype(jnp.float32) + other_coef * other_rows.astype(
            jnp.float32
        )
        held_rows = merged.astype(jnp.bfloat16)
    combined = held_rows.astype(jnp.float32).reshape(momentum.shape)
    new_momentum = 0.9 * momentum + 0.0625 * combined
    new_weights = master - 0.02 * new_momentum
    return (passed[None, None], new_momentum, new_weights)

MESH = pl.DeviceIdType.MESH
F32 = jnp.float32
BF16 = jnp.bfloat16


def chunk_rows(channels):
    return next(rows for rows in (64, 48, 32, 16) if channels % rows == 0)


def fold(product):
    return jnp.sum(product.reshape(-1, 8, product.shape[-1]), axis=0)


def pair_dots(lower, upper, rows_total, rows):
    channels = lower.shape[-1]

    def step(i, sums):
        here = pl.ds(pl.multiple_of(i * rows, rows), rows)
        a, b = lower[here, :].astype(F32), upper[here, :].astype(F32)
        return sums[0] + fold(a * a), sums[1] + fold(b * b), sums[2] + fold(a * b)

    zero = jnp.zeros((8, channels), F32)
    aa, bb, ab = lax.fori_loop(0, rows_total // rows, step, (zero, zero, zero))
    aa, bb, ab = jnp.sum(aa), jnp.sum(bb), jnp.sum(ab)
    return 1.0 - ab / (2.0 * aa + EPS), 1.0 - ab / (2.0 * bb + EPS)


def pair_merge(lower, upper, target, coefs, rows_total, rows):
    def step(i, carry):
        here = pl.ds(pl.multiple_of(i * rows, rows), rows)
        a, b = lower[here, :].astype(F32), upper[here, :].astype(F32)
        target[here, :] = (coefs[0] * a + coefs[1] * b).astype(BF16)
        return carry

    lax.fori_loop(0, rows_total // rows, step, 0)


def kernel(
    sections, replicas, cols,
    act_ref, pre_ref, up_ref, weights_hbm, master_hbm, momentum_hbm,
    passed_ref, new_mom_ref, new_w_ref,
    factors, shifted, xt, kernel_v, igrad, pair_w, merged, master_v, momentum_v,
    send_sem, recv_sem, pass_sem, load_sem,
):
    pixels, channels = act_ref.shape
    rows_total = kernel_v.shape[0]
    rows = chunk_rows(channels)
    pipe, rep = lax.axis_index("pipe"), lax.axis_index("rep")
    chain = replicas // 2
    z, y = rep // 2, rep % 2
    other = z * 2 + 1 - y

    barrier = pltpu.get_barrier_semaphore()

    def greet(cond, device):
        @pl.when(cond)
        def _():
            pl.semaphore_signal(barrier, inc=1, device_id=device, device_id_type=MESH)

    pl.semaphore_signal(barrier, inc=1, device_id=(pipe, other), device_id_type=MESH)
    greet(z > 0, (pipe, rep - 2))
    greet(z < chain - 1, (pipe, rep + 2))
    greet(pipe < sections - 1, (pipe + 1, rep))

    loads = [
        pltpu.make_async_copy(src, dst, load_sem.at[i])
        for i, (src, dst) in enumerate(
            ((weights_hbm, kernel_v), (master_hbm, master_v), (momentum_hbm, momentum_v))
        )
    ]
    for load in loads:
        load.start()

    z_f = pre_ref[...].astype(F32)
    sig = jax.nn.sigmoid(z_f)
    factors[rep, 1] = (up_ref[...].astype(F32) * sig * (1.0 + z_f * (1.0 - sig))).astype(BF16)
    factors[rep, 0] = act_ref[...]

    edge = jnp.zeros((cols, channels), BF16)
    for j in range(3):
        shifted[j, pl.ds(0, cols), :] = edge
        shifted[j, pl.ds(cols + pixels, cols), :] = edge

    def spread(block):
        grad = factors[block, 1].astype(F32)
        column = lax.broadcasted_iota(jnp.int32, (pixels, channels), 0) % cols
        here = pl.ds(cols, pixels)
        shifted[0, here, :] = jnp.where(
            column < cols - 1, pltpu.roll(grad, pixels - 1, 0), 0.0
        ).astype(BF16)
        shifted[1, here, :] = factors[block, 1]
        shifted[2, here, :] = jnp.where(column > 0, pltpu.roll(grad, 1, 0), 0.0).astype(BF16)

    def tap(i, j):
        return shifted[j, pl.ds((2 - i) * cols, pixels), :]

    met = 1 + (z > 0).astype(jnp.int32) + (z < chain - 1).astype(jnp.int32)
    pl.semaphore_wait(barrier, met + (pipe > 0).astype(jnp.int32))

    def copy_of(block, half, way, target):
        return pltpu.make_async_remote_copy(
            src_ref=factors.at[block, half],
            dst_ref=factors.at[block, half],
            send_sem=send_sem.at[way, block, half],
            recv_sem=recv_sem.at[block, half],
            device_id=(pipe, target),
            device_id_type=MESH,
        )

    def ways(source):
        return (
            (0, (source <= z) & (z < chain - 1), jnp.minimum(rep + 2, replicas - 1)),
            (1, (source >= z) & (z > 0), jnp.maximum(rep - 2, 0)),
        )

    def order(k):
        if k == 0:
            return z
        short = jnp.minimum(z, chain - 1 - z)
        near = z - (k + 1) // 2 if k % 2 else z + k // 2
        far = jnp.where(z <= chain - 1 - z, k, chain - 1 - k)
        return jnp.where(k <= 2 * short, near, far)

    sources = [order(k) for k in range(chain)]

    def forward(k):
        source = sources[k]
        block = source * 2 + y
        for half in range(2):
            if k:
                copy_of(block, half, 2, other).wait_recv()
            for way, cond, target in ways(source):
                @pl.when(cond)
                def _():
                    copy_of(block, half, way, target).start()
            copy_of(block, half, 2, other).start()

    def replica_grad(slot, block):
        spread(block)
        xt[...] = factors[block, 0].T
        for i in range(3):
            for j in range(3):
                grad = jnp.dot(xt[...], tap(i, j), preferred_element_type=F32)
                pair_w[slot, pl.ds((i * 3 + j) * channels, channels), :] = grad.astype(BF16)

    def process(k):
        source = sources[k]

        def one(slot, carry):
            block = source * 2 + jnp.where(slot == 0, y, 1 - y)

            @pl.when(slot == 1)
            def _():
                for half in range(2):
                    copy_of(block, half, 2, other).wait_recv()

            replica_grad(jnp.where(slot == 0, y, 1 - y), block)
            return carry

        lax.fori_loop(0, 2, one, 0)
        coefs = pair_dots(pair_w.at[0], pair_w.at[1], rows_total, rows)
        pair_merge(pair_w.at[0], pair_w.at[1], merged.at[source], coefs, rows_total, rows)

    forward(0)

    spread(rep)
    loads[0].wait()
    total = jnp.zeros((pixels, channels), F32)
    for i in range(3):
        for j in range(3):
            total = total + lax.dot_general(
                tap(i, j),
                kernel_v[pl.ds((i * 3 + j) * channels, channels), :],
                (((1,), (1,)), ((), ())),
                preferred_element_type=F32,
            )
    igrad[...] = total.astype(BF16)

    @pl.when(pipe == sections - 1)
    def _():
        passed_ref[...] = jnp.zeros_like(passed_ref)

    passing = pltpu.make_async_remote_copy(
        src_ref=igrad,
        dst_ref=passed_ref,
        send_sem=pass_sem.at[0],
        recv_sem=pass_sem.at[1],
        device_id=(jnp.maximum(pipe - 1, 0), rep),
        device_id_type=MESH,
    )

    for k in range(1, chain):
        forward(k)
        if k == 1:
            @pl.when(pipe > 0)
            def _():
                passing.start()
        process(k - 1)
    if chain == 1:
        @pl.when(pipe > 0)
        def _():
            passing.start()
    process(chain - 1)

    stride = 1
    while stride * 2 < chain:
        for low in range(0, chain, stride * 2):
            pair = merged.at[low], merged.at[low + stride]
            coefs = pair_dots(*pair, rows_total, rows)
            pair_merge(*pair, merged.at[low], coefs, rows_total, rows)
        stride *= 2
    for load in loads[1:]:
        load.wait()
    own_rows = rows_total // replicas
    own = pl.ds(pl.multiple_of(rep * own_rows, own_rows), own_rows)
    if stride < chain:
        coefs = pair_dots(merged.at[0], merged.at[stride], rows_total, rows)
        final = coefs[0] * merged[0, own, :].astype(F32) + coefs[1] * merged[stride, own, :].astype(F32)
        final = final.astype(BF16).astype(F32)
    else:
        final = merged[0, own, :].astype(F32)
    lanes = momentum_v.shape[-1]
    groups = channels // lanes
    for g in range(groups):
        at = pl.ds(g, own_rows, stride=groups)
        momentum = 0.9 * momentum_v[at, :] + 0.0625 * final[:, g * lanes : (g + 1) * lanes]
        new_mom_ref[at, :] = momentum
        new_w_ref[at, :] = master_v[at, :] - 0.02 * momentum

    for k in range(chain):
        source = sources[k]
        block = source * 2 + y
        for half in range(2):
            for way, cond, target in ways(source):
                @pl.when(cond)
                def _():
                    copy_of(block, half, way, target).wait_send()
            copy_of(block, half, 2, other).wait_send()

    @pl.when(pipe > 0)
    def _():
        passing.wait_send()

    @pl.when(pipe < sections - 1)
    def _():
        passing.wait_recv()


def factor_body(sections, replicas, activations, preactivation, upstream, weights, master, momentum):
    tile = activations.shape[3:]
    cols, channels = tile[1], tile[2]
    pixels = tile[0] * cols
    taps_rows = weights.shape[1]
    lanes = 128
    flat = (momentum.shape[2] // lanes, lanes)
    small, big = pl.BlockSpec(memory_space=pltpu.VMEM), pl.BlockSpec(memory_space=pl.ANY)
    passed, new_momentum, new_weights = pl.pallas_call(
        functools.partial(kernel, sections, replicas, cols),
        out_shape=(
            jax.ShapeDtypeStruct((pixels, channels), BF16),
            jax.ShapeDtypeStruct(flat, F32),
            jax.ShapeDtypeStruct(flat, F32),
        ),
        in_specs=[small, small, small, big, big, big],
        out_specs=(small, small, small),
        scratch_shapes=[
            pltpu.VMEM((replicas, 2, pixels, channels), BF16),
            pltpu.VMEM((3, pixels + 2 * cols, channels), BF16),
            pltpu.VMEM((channels, pixels), BF16),
            pltpu.VMEM((taps_rows, channels), BF16),
            pltpu.VMEM((pixels, channels), BF16),
            pltpu.VMEM((2, taps_rows, channels), BF16),
            pltpu.VMEM((replicas // 2, taps_rows, channels), BF16),
            pltpu.VMEM(flat, F32),
            pltpu.VMEM(flat, F32),
            pltpu.SemaphoreType.DMA((3, replicas, 2)),
            pltpu.SemaphoreType.DMA((replicas, 2)),
            pltpu.SemaphoreType.DMA((2,)),
            pltpu.SemaphoreType.DMA((3,)),
        ],
        compiler_params=pltpu.CompilerParams(
            collective_id=0, has_side_effects=True, vmem_limit_bytes=56 * 1024 * 1024
        ),
    )(
        activations.reshape(pixels, channels),
        preactivation.reshape(pixels, channels),
        upstream.reshape(pixels, channels),
        weights[0],
        master.reshape(flat),
        momentum.reshape(flat),
    )
    return (
        passed.reshape(activations.shape),
        new_momentum.reshape(momentum.shape),
        new_weights.reshape(master.shape),
    )


def pick(sections, replicas, *arrays):
    activations, weights, momentum = arrays[0], arrays[3], arrays[5]
    factor = 2 * activations.size
    fits = (
        replicas >= 2
        and activations.shape[2] == 1
        and (replicas - 1) * factor <= 2 * weights.size
        and activations.shape[4] % 16 == 0
        and activations.shape[5] % 128 == 0
        and (weights.shape[1] // replicas) % 16 == 0
        and momentum.shape[2] % 1024 == 0
    )
    return factor_body(sections, replicas, *arrays) if fits else body(*arrays)


def solution(mesh):
    return jax.shard_map(
        functools.partial(pick, mesh.shape["pipe"], mesh.shape["rep"]),
        mesh=mesh,
        in_specs=(
            P("pipe", "rep", None, None, None, None),
            P("pipe", "rep", None, None, None, None),
            P("pipe", "rep", None, None, None, None),
            P("pipe", None, None),
            P("pipe", "rep", None),
            P("pipe", "rep", None),
        ),
        out_specs=(
            P("pipe", "rep", None, None, None, None),
            P("pipe", "rep", None),
            P("pipe", "rep", None),
        ),
        check_vma=False,
    )
```

```python
import functools

import jax
import jax.numpy as jnp
from jax import lax
from jax.experimental import pallas as pl
from jax.experimental.pallas import tpu as pltpu
from jax.sharding import PartitionSpec as P

EPS = 1e-06


def swapped(shard, axis, stride):
    return lax.ppermute(shard, axis, [(i, i ^ 1 << stride) for i in range(lax.axis_size(axis))])


def from_behind(shard, axis, by):
    count = lax.axis_size(axis)
    pairs = [(i, i + by) for i in range(count) if 0 <= i + by < count]
    return lax.ppermute(shard, axis, pairs)


def shifted_patches(tile_data, flipped):
    frames, tile_rows, tile_cols, channels = tile_data.shape
    padded = jnp.pad(tile_data, ((0, 0), (1, 1), (1, 1), (0, 0)))
    if flipped:
        offsets = [(2 - row_off, 2 - col_off) for row_off in range(3) for col_off in range(3)]
    else:
        offsets = [(row_off, col_off) for row_off in range(3) for col_off in range(3)]
    pieces = [
        padded[:, first : first + tile_rows, second : second + tile_cols, :]
        for first, second in offsets
    ]
    return jnp.concatenate(pieces, axis=-1).reshape(frames * tile_rows * tile_cols, 9 * channels)


def local_backward(tile_data, preact_tile, upstream_tile, kernel):
    frames, tile_rows, tile_cols, channels = tile_data.shape
    pre_float = preact_tile.astype(jnp.float32)
    sigmoid_val = jax.nn.sigmoid(pre_float)
    local_grad = (
        upstream_tile.astype(jnp.float32) * sigmoid_val * (1.0 + pre_float * (1.0 - sigmoid_val))
    ).astype(jnp.bfloat16)
    flat_grad = local_grad.reshape(-1, channels)
    patches = shifted_patches(tile_data, False)
    weight_grad = lax.dot_general(
        patches, flat_grad, (((0,), (0,)), ((), ())), preferred_element_type=jnp.float32
    ).astype(jnp.bfloat16)
    grad_patches = shifted_patches(local_grad, True).reshape(-1, 9, channels)
    kernel_taps = kernel.reshape(9, channels, channels)
    summed = lax.dot_general(
        grad_patches, kernel_taps, (((1, 2), (0, 2)), ((), ())), preferred_element_type=jnp.float32
    )
    return (
        weight_grad,
        summed.astype(jnp.bfloat16).reshape(frames, tile_rows, tile_cols, channels),
    )


def group_sum(partials, sum_bits):
    for bit_number in range(sum_bits):
        partials = partials + swapped(partials, "rep", bit_number)
    return partials


def body(activations, preactivation, upstream, weights, master, momentum):
    weight_grad, input_grad = local_backward(
        activations[0, 0], preactivation[0, 0], upstream[0, 0], weights[0]
    )
    passed = from_behind(input_grad, "pipe", -1)
    replicas = lax.axis_size("rep")
    level_count = replicas.bit_length() - 1
    rep_index = lax.axis_index("rep")
    held_rows = weight_grad.reshape(replicas, -1)
    for level_num in range(level_count):
        is_lower = jnp.right_shift(rep_index, level_num) & 1 == 0
        paired = held_rows.reshape(-1, 2, held_rows.shape[1])
        keep_rows = jnp.where(is_lower, paired[:, 0], paired[:, 1])
        give_rows = jnp.where(is_lower, paired[:, 1], paired[:, 0])
        other_rows = swapped(give_rows, "rep", level_num)
        keep_float = keep_rows.astype(jnp.float32)
        other_float = other_rows.astype(jnp.float32)
        keep_sq = jnp.sum(keep_float * keep_float)
        other_sq = jnp.sum(other_float * other_float)
        partials = jnp.stack(
            [
                jnp.where(is_lower, keep_sq, other_sq),
                jnp.where(is_lower, other_sq, keep_sq),
                jnp.sum(keep_float * other_float),
            ]
        )
        sum_bits = level_num + 1
        partials = group_sum(partials, sum_bits)
        lower_coef = 1.0 - partials[2] / (2.0 * partials[0] + EPS)
        upper_coef = 1.0 - partials[2] / (2.0 * partials[1] + EPS)
        keep_coef = jnp.where(is_lower, lower_coef, upper_coef)
        other_coef = jnp.where(is_lower, upper_coef, lower_coef)
        merged = keep_coef * keep_rows.astype(jnp.float32) + other_coef * other_rows.astype(
            jnp.float32
        )
        held_rows = merged.astype(jnp.bfloat16)
    combined = held_rows.astype(jnp.float32).reshape(momentum.shape)
    new_momentum = 0.9 * momentum + 0.0625 * combined
    new_weights = master - 0.02 * new_momentum
    return (passed[None, None], new_momentum, new_weights)

MESH = pl.DeviceIdType.MESH
F32 = jnp.float32
BF16 = jnp.bfloat16


def chunk_rows(channels):
    return next(rows for rows in (64, 48, 32, 16) if channels % rows == 0)


def fold(product):
    return jnp.sum(product.reshape(-1, 8, product.shape[-1]), axis=0)


def coefs_of(lower_sq, upper_sq, cross):
    aa, bb, ab = jnp.sum(lower_sq), jnp.sum(upper_sq), jnp.sum(cross)
    return 1.0 - ab / (2.0 * aa + EPS), 1.0 - ab / (2.0 * bb + EPS)


def pair_merge(lower, upper, target, coefs, against, rows_total, rows):
    channels = lower.shape[-1]

    def step(i, sums):
        here = pl.ds(pl.multiple_of(i * rows, rows), rows)
        a, b = lower[here, :].astype(F32), upper[here, :].astype(F32)
        new = (coefs[0] * a + coefs[1] * b).astype(BF16)
        target[here, :] = new
        if against is None:
            return sums
        new, next_one = new.astype(F32), against[here, :].astype(F32)
        return (
            sums[0] + fold(new * new),
            sums[1] + fold(next_one * next_one),
            sums[2] + fold(new * next_one),
        )

    zero = jnp.zeros((8, channels), F32)
    init = () if against is None else (zero, zero, zero)
    sums = lax.fori_loop(0, rows_total // rows, step, init)
    return None if against is None else coefs_of(*sums)


def kernel(
    sections, replicas, cols,
    act_ref, pre_ref, up_ref, weights_hbm,
    passed_ref, combined_ref,
    factors, shifted, xt, kernel_v, igrad, pair_w, merged,
    send_sem, recv_sem, pass_sem, load_sem,
):
    pixels, channels = act_ref.shape
    rows_total = kernel_v.shape[0]
    rows = chunk_rows(channels)
    pipe, rep = lax.axis_index("pipe"), lax.axis_index("rep")
    chain = replicas // 2
    z, y = rep // 2, rep % 2
    other = z * 2 + 1 - y

    barrier = pltpu.get_barrier_semaphore()

    def greet(cond, device):
        @pl.when(cond)
        def _():
            pl.semaphore_signal(barrier, inc=1, device_id=device, device_id_type=MESH)

    pl.semaphore_signal(barrier, inc=1, device_id=(pipe, other), device_id_type=MESH)
    greet(z > 0, (pipe, rep - 2))
    greet(z < chain - 1, (pipe, rep + 2))
    greet(pipe < sections - 1, (pipe + 1, rep))

    load = pltpu.make_async_copy(weights_hbm, kernel_v, load_sem)
    load.start()
    factors[rep, 0] = act_ref[...]

    edge = jnp.zeros((cols, channels), BF16)
    for j in range(3):
        shifted[j, pl.ds(0, cols), :] = edge
        shifted[j, pl.ds(cols + pixels, cols), :] = edge

    def spread(block):
        grad = factors[block, 1].astype(F32)
        column = lax.broadcasted_iota(jnp.int32, (pixels, channels), 0) % cols
        here = pl.ds(cols, pixels)
        shifted[0, here, :] = jnp.where(
            column < cols - 1, pltpu.roll(grad, pixels - 1, 0), 0.0
        ).astype(BF16)
        shifted[1, here, :] = factors[block, 1]
        shifted[2, here, :] = jnp.where(column > 0, pltpu.roll(grad, 1, 0), 0.0).astype(BF16)

    def tap(i, j):
        return shifted[j, pl.ds((2 - i) * cols, pixels), :]

    met = 1 + (z > 0).astype(jnp.int32) + (z < chain - 1).astype(jnp.int32)
    pl.semaphore_wait(barrier, met + (pipe > 0).astype(jnp.int32))

    def copy_of(block, half, way, target):
        return pltpu.make_async_remote_copy(
            src_ref=factors.at[block, half],
            dst_ref=factors.at[block, half],
            send_sem=send_sem.at[way, block, half],
            recv_sem=recv_sem.at[block, half],
            device_id=(pipe, target),
            device_id_type=MESH,
        )

    def ways(source):
        return (
            (0, (source <= z) & (z < chain - 1), jnp.minimum(rep + 2, replicas - 1)),
            (1, (source >= z) & (z > 0), jnp.maximum(rep - 2, 0)),
        )

    def order(k):
        if k == 0:
            return z
        size = 1 << (k.bit_length() - 1)
        step, group = k - size, z // size
        return jnp.where(
            group % 2 == 0, (group + 1) * size + step, group * size - 1 - step
        )

    sources = [order(k) for k in range(chain)]

    def forward(k, halves=(0, 1)):
        source = sources[k]
        block = source * 2 + y
        for half in halves:
            if k:
                copy_of(block, half, 2, other).wait_recv()
            for way, cond, target in ways(source):
                @pl.when(cond)
                def _():
                    copy_of(block, half, way, target).start()
            copy_of(block, half, 2, other).start()

    def replica_grad(slot, block):
        spread(block)
        xt[...] = factors[block, 0].T
        own_sq = jnp.zeros((8, channels), F32)
        cross = jnp.zeros((8, channels), F32)
        for i in range(3):
            for j in range(3):
                here = pl.ds((i * 3 + j) * channels, channels)
                grad = jnp.dot(xt[...], tap(i, j), preferred_element_type=F32).astype(BF16)
                pair_w[slot, here, :] = grad
                grad = grad.astype(F32)
                own_sq = own_sq + fold(grad * grad)
                if slot:
                    cross = cross + fold(grad * pair_w[0, here, :].astype(F32))
        return own_sq, cross

    stack = []

    def process(k):
        source = sources[k]
        first_sq, _ = replica_grad(0, source * 2 + y)
        for half in range(2):
            copy_of(source * 2 + 1 - y, half, 2, other).wait_recv()
        second_sq, cross = replica_grad(1, source * 2 + 1 - y)
        coefs = coefs_of(first_sq, second_sq, cross)
        lower, upper, target = pair_w.at[0], pair_w.at[1], source
        rest = k + 1
        while True:
            against = merged.at[stack[-1]] if rest % 2 == 0 else None
            coefs = pair_merge(lower, upper, merged.at[target], coefs, against, rows_total, rows)
            if against is None:
                stack.append(target)
                return None
            lower, upper = merged.at[target], against
            target = stack.pop()
            rest //= 2
            if k == chain - 1 and not stack:
                return lower, upper, coefs

    forward(0, (0,))
    z_f = pre_ref[...].astype(F32)
    sig = jax.nn.sigmoid(z_f)
    factors[rep, 1] = (up_ref[...].astype(F32) * sig * (1.0 + z_f * (1.0 - sig))).astype(BF16)
    spread(rep)
    forward(0, (1,))
    load.wait()
    total = jnp.zeros((pixels, channels), F32)
    for i in range(3):
        for j in range(3):
            total = total + lax.dot_general(
                tap(i, j),
                kernel_v[pl.ds((i * 3 + j) * channels, channels), :],
                (((1,), (1,)), ((), ())),
                preferred_element_type=F32,
            )
    igrad[...] = total.astype(BF16)

    @pl.when(pipe == sections - 1)
    def _():
        passed_ref[...] = jnp.zeros_like(passed_ref)

    passing = pltpu.make_async_remote_copy(
        src_ref=igrad,
        dst_ref=passed_ref,
        send_sem=pass_sem.at[0],
        recv_sem=pass_sem.at[1],
        device_id=(jnp.maximum(pipe - 1, 0), rep),
        device_id_type=MESH,
    )

    for k in range(1, chain):
        forward(k)
        if k == 1:
            @pl.when(pipe > 0)
            def _():
                passing.start()
        process(k - 1)
    lower, upper, coefs = process(chain - 1)

    own_rows = rows_total // replicas
    own = pl.ds(pl.multiple_of(rep * own_rows, own_rows), own_rows)
    final = coefs[0] * lower[own, :].astype(F32) + coefs[1] * upper[own, :].astype(F32)
    combined_ref[...] = final.astype(BF16)

    for k in range(chain):
        source = sources[k]
        block = source * 2 + y
        for half in range(2):
            for way, cond, target in ways(source):
                @pl.when(cond)
                def _():
                    copy_of(block, half, way, target).wait_send()
            copy_of(block, half, 2, other).wait_send()

    @pl.when(pipe > 0)
    def _():
        passing.wait_send()

    @pl.when(pipe < sections - 1)
    def _():
        passing.wait_recv()


def update(combined, master, momentum, passed_in, new_momentum, new_weights, passed_out):
    own_rows, channels = combined.shape
    lanes = momentum.shape[-1]
    groups = channels // lanes
    passed_out[...] = passed_in[...]
    for g in range(groups):
        at = pl.ds(g, own_rows, stride=groups)
        part = combined[:, g * lanes : (g + 1) * lanes].astype(F32)
        moved = 0.9 * momentum[at, :] + 0.0625 * part
        new_momentum[at, :] = moved
        new_weights[at, :] = master[at, :] - 0.02 * moved


def factor_body(sections, replicas, activations, preactivation, upstream, weights, master, momentum):
    tile = activations.shape[3:]
    cols, channels = tile[1], tile[2]
    pixels = tile[0] * cols
    taps_rows = weights.shape[1]
    lanes = 128
    flat = (momentum.shape[2] // lanes, lanes)
    small, big = pl.BlockSpec(memory_space=pltpu.VMEM), pl.BlockSpec(memory_space=pl.ANY)
    passed, combined = pl.pallas_call(
        functools.partial(kernel, sections, replicas, cols),
        out_shape=(
            jax.ShapeDtypeStruct((pixels, channels), BF16),
            jax.ShapeDtypeStruct((taps_rows // replicas, channels), BF16),
        ),
        in_specs=[small, small, small, big],
        out_specs=(small, small),
        scratch_shapes=[
            pltpu.VMEM((replicas, 2, pixels, channels), BF16),
            pltpu.VMEM((3, pixels + 2 * cols, channels), BF16),
            pltpu.VMEM((channels, pixels), BF16),
            pltpu.VMEM((taps_rows, channels), BF16),
            pltpu.VMEM((pixels, channels), BF16),
            pltpu.VMEM((2, taps_rows, channels), BF16),
            pltpu.VMEM((replicas // 2, taps_rows, channels), BF16),
            pltpu.SemaphoreType.DMA((3, replicas, 2)),
            pltpu.SemaphoreType.DMA((replicas, 2)),
            pltpu.SemaphoreType.DMA((2,)),
            pltpu.SemaphoreType.DMA,
        ],
        compiler_params=pltpu.CompilerParams(
            collective_id=0, has_side_effects=True, vmem_limit_bytes=56 * 1024 * 1024
        ),
    )(
        activations.reshape(pixels, channels),
        preactivation.reshape(pixels, channels),
        upstream.reshape(pixels, channels),
        weights[0],
    )
    new_momentum, new_weights, passed = pl.pallas_call(
        update,
        out_shape=(
            jax.ShapeDtypeStruct(flat, F32),
            jax.ShapeDtypeStruct(flat, F32),
            jax.ShapeDtypeStruct((pixels, channels), BF16),
        ),
        in_specs=[small] * 4,
        out_specs=(small,) * 3,
    )(combined, master.reshape(flat), momentum.reshape(flat), passed)
    return (
        passed.reshape(activations.shape),
        new_momentum.reshape(momentum.shape),
        new_weights.reshape(master.shape),
    )


def pick(sections, replicas, *arrays):
    activations, weights, momentum = arrays[0], arrays[3], arrays[5]
    factor = 2 * activations.size
    fits = (
        replicas >= 4
        and replicas & (replicas - 1) == 0
        and activations.shape[2] == 1
        and (replicas - 1) * factor <= 2 * weights.size
        and activations.shape[4] % 16 == 0
        and activations.shape[5] % 128 == 0
        and (weights.shape[1] // replicas) % 16 == 0
        and momentum.shape[2] % 1024 == 0
    )
    return factor_body(sections, replicas, *arrays) if fits else body(*arrays)


def solution(mesh):
    return jax.shard_map(
        functools.partial(pick, mesh.shape["pipe"], mesh.shape["rep"]),
        mesh=mesh,
        in_specs=(
            P("pipe", "rep", None, None, None, None),
            P("pipe", "rep", None, None, None, None),
            P("pipe", "rep", None, None, None, None),
            P("pipe", None, None),
            P("pipe", "rep", None),
            P("pipe", "rep", None),
        ),
        out_specs=(
            P("pipe", "rep", None, None, None, None),
            P("pipe", "rep", None),
            P("pipe", "rep", None),
        ),
        check_vma=False,
    )
```

```python
import functools

import jax
import jax.numpy as jnp
from jax import lax
from jax.experimental import pallas as pl
from jax.experimental.pallas import tpu as pltpu
from jax.sharding import PartitionSpec as P

EPS = 1e-06


def swapped(shard, axis, stride):
    return lax.ppermute(shard, axis, [(i, i ^ 1 << stride) for i in range(lax.axis_size(axis))])


def from_behind(shard, axis, by):
    count = lax.axis_size(axis)
    pairs = [(i, i + by) for i in range(count) if 0 <= i + by < count]
    return lax.ppermute(shard, axis, pairs)


def shifted_patches(tile_data, flipped):
    frames, tile_rows, tile_cols, channels = tile_data.shape
    padded = jnp.pad(tile_data, ((0, 0), (1, 1), (1, 1), (0, 0)))
    if flipped:
        offsets = [(2 - row_off, 2 - col_off) for row_off in range(3) for col_off in range(3)]
    else:
        offsets = [(row_off, col_off) for row_off in range(3) for col_off in range(3)]
    pieces = [
        padded[:, first : first + tile_rows, second : second + tile_cols, :]
        for first, second in offsets
    ]
    return jnp.concatenate(pieces, axis=-1).reshape(frames * tile_rows * tile_cols, 9 * channels)


def local_backward(tile_data, preact_tile, upstream_tile, kernel):
    frames, tile_rows, tile_cols, channels = tile_data.shape
    pre_float = preact_tile.astype(jnp.float32)
    sigmoid_val = jax.nn.sigmoid(pre_float)
    local_grad = (
        upstream_tile.astype(jnp.float32) * sigmoid_val * (1.0 + pre_float * (1.0 - sigmoid_val))
    ).astype(jnp.bfloat16)
    flat_grad = local_grad.reshape(-1, channels)
    patches = shifted_patches(tile_data, False)
    weight_grad = lax.dot_general(
        patches, flat_grad, (((0,), (0,)), ((), ())), preferred_element_type=jnp.float32
    ).astype(jnp.bfloat16)
    grad_patches = shifted_patches(local_grad, True).reshape(-1, 9, channels)
    kernel_taps = kernel.reshape(9, channels, channels)
    summed = lax.dot_general(
        grad_patches, kernel_taps, (((1, 2), (0, 2)), ((), ())), preferred_element_type=jnp.float32
    )
    return (
        weight_grad,
        summed.astype(jnp.bfloat16).reshape(frames, tile_rows, tile_cols, channels),
    )


def group_sum(partials, sum_bits):
    for bit_number in range(sum_bits):
        partials = partials + swapped(partials, "rep", bit_number)
    return partials


def body(activations, preactivation, upstream, weights, master, momentum):
    weight_grad, input_grad = local_backward(
        activations[0, 0], preactivation[0, 0], upstream[0, 0], weights[0]
    )
    passed = from_behind(input_grad, "pipe", -1)
    replicas = lax.axis_size("rep")
    level_count = replicas.bit_length() - 1
    rep_index = lax.axis_index("rep")
    held_rows = weight_grad.reshape(replicas, -1)
    for level_num in range(level_count):
        is_lower = jnp.right_shift(rep_index, level_num) & 1 == 0
        paired = held_rows.reshape(-1, 2, held_rows.shape[1])
        keep_rows = jnp.where(is_lower, paired[:, 0], paired[:, 1])
        give_rows = jnp.where(is_lower, paired[:, 1], paired[:, 0])
        other_rows = swapped(give_rows, "rep", level_num)
        keep_float = keep_rows.astype(jnp.float32)
        other_float = other_rows.astype(jnp.float32)
        keep_sq = jnp.sum(keep_float * keep_float)
        other_sq = jnp.sum(other_float * other_float)
        partials = jnp.stack(
            [
                jnp.where(is_lower, keep_sq, other_sq),
                jnp.where(is_lower, other_sq, keep_sq),
                jnp.sum(keep_float * other_float),
            ]
        )
        sum_bits = level_num + 1
        partials = group_sum(partials, sum_bits)
        lower_coef = 1.0 - partials[2] / (2.0 * partials[0] + EPS)
        upper_coef = 1.0 - partials[2] / (2.0 * partials[1] + EPS)
        keep_coef = jnp.where(is_lower, lower_coef, upper_coef)
        other_coef = jnp.where(is_lower, upper_coef, lower_coef)
        merged = keep_coef * keep_rows.astype(jnp.float32) + other_coef * other_rows.astype(
            jnp.float32
        )
        held_rows = merged.astype(jnp.bfloat16)
    combined = held_rows.astype(jnp.float32).reshape(momentum.shape)
    new_momentum = 0.9 * momentum + 0.0625 * combined
    new_weights = master - 0.02 * new_momentum
    return (passed[None, None], new_momentum, new_weights)

MESH = pl.DeviceIdType.MESH
F32 = jnp.float32
BF16 = jnp.bfloat16


def chunk_rows(channels):
    return next(rows for rows in (64, 48, 32, 16) if channels % rows == 0)


def fold(product):
    return jnp.sum(product.reshape(-1, 8, product.shape[-1]), axis=0)


def coefs_of(lower_sq, upper_sq, cross):
    aa, bb, ab = jnp.sum(lower_sq), jnp.sum(upper_sq), jnp.sum(cross)
    return 1.0 - ab / (2.0 * aa + EPS), 1.0 - ab / (2.0 * bb + EPS)


def pair_merge(lower, upper, target, coefs, against, rows_total, rows):
    channels = lower.shape[-1]

    def step(i, sums):
        here = pl.ds(pl.multiple_of(i * rows, rows), rows)
        a, b = lower[here, :].astype(F32), upper[here, :].astype(F32)
        new = (coefs[0] * a + coefs[1] * b).astype(BF16)
        target[here, :] = new
        if against is None:
            return sums
        new, next_one = new.astype(F32), against[here, :].astype(F32)
        return (
            sums[0] + fold(new * new),
            sums[1] + fold(next_one * next_one),
            sums[2] + fold(new * next_one),
        )

    zero = jnp.zeros((8, channels), F32)
    init = () if against is None else (zero, zero, zero)
    count = rows_total // rows
    sums = lax.fori_loop(0, count, step, init, unroll=next(n for n in (3, 2, 1) if count % n == 0))
    return None if against is None else coefs_of(*sums)


def kernel(
    sections, replicas, cols,
    act_ref, pre_ref, up_ref, weights_hbm,
    passed_ref, combined_ref,
    factors, shifted, xt, kernel_v, igrad, pair_w, merged,
    send_sem, recv_sem, pass_sem, load_sem,
):
    pixels, channels = act_ref.shape
    rows_total = kernel_v.shape[0]
    rows = chunk_rows(channels)
    pipe, rep = lax.axis_index("pipe"), lax.axis_index("rep")
    chain = replicas // 2
    z, y = rep // 2, rep % 2
    other = z * 2 + 1 - y

    barrier = pltpu.get_barrier_semaphore()

    def greet(cond, device):
        @pl.when(cond)
        def _():
            pl.semaphore_signal(barrier, inc=1, device_id=device, device_id_type=MESH)

    pl.semaphore_signal(barrier, inc=1, device_id=(pipe, other), device_id_type=MESH)
    greet(z > 0, (pipe, rep - 2))
    greet(z < chain - 1, (pipe, rep + 2))
    greet(pipe < sections - 1, (pipe + 1, rep))

    load = pltpu.make_async_copy(weights_hbm, kernel_v, load_sem)
    load.start()
    factors[rep, 0] = act_ref[...]

    edge = jnp.zeros((cols, channels), BF16)
    for j in range(3):
        shifted[j, pl.ds(0, cols), :] = edge
        shifted[j, pl.ds(cols + pixels, cols), :] = edge

    def spread(block):
        grad = factors[block, 1].astype(F32)
        column = lax.broadcasted_iota(jnp.int32, (pixels, channels), 0) % cols
        here = pl.ds(cols, pixels)
        shifted[0, here, :] = jnp.where(
            column < cols - 1, pltpu.roll(grad, pixels - 1, 0), 0.0
        ).astype(BF16)
        shifted[1, here, :] = factors[block, 1]
        shifted[2, here, :] = jnp.where(column > 0, pltpu.roll(grad, 1, 0), 0.0).astype(BF16)

    def tap(i, j):
        return shifted[j, pl.ds((2 - i) * cols, pixels), :]

    met = 1 + (z > 0).astype(jnp.int32) + (z < chain - 1).astype(jnp.int32)
    pl.semaphore_wait(barrier, met + (pipe > 0).astype(jnp.int32))

    def copy_of(block, half, way, target):
        return pltpu.make_async_remote_copy(
            src_ref=factors.at[block, half],
            dst_ref=factors.at[block, half],
            send_sem=send_sem.at[way, block, half],
            recv_sem=recv_sem.at[block, half],
            device_id=(pipe, target),
            device_id_type=MESH,
        )

    def ways(source):
        return (
            (0, (source <= z) & (z < chain - 1), jnp.minimum(rep + 2, replicas - 1)),
            (1, (source >= z) & (z > 0), jnp.maximum(rep - 2, 0)),
        )

    def order(k):
        if k == 0:
            return z
        size = 1 << (k.bit_length() - 1)
        step, group = k - size, z // size
        return jnp.where(
            group % 2 == 0, (group + 1) * size + step, group * size - 1 - step
        )

    sources = [order(k) for k in range(chain)]

    def forward(k, halves=(0, 1)):
        source = sources[k]
        block = source * 2 + y
        for half in halves:
            if k:
                copy_of(block, half, 2, other).wait_recv()
            for way, cond, target in ways(source):
                @pl.when(cond)
                def _():
                    copy_of(block, half, way, target).start()
            copy_of(block, half, 2, other).start()

    def replica_grad(slot, block):
        spread(block)
        xt[...] = factors[block, 0].T
        own_sq = jnp.zeros((8, channels), F32)
        cross = jnp.zeros((8, channels), F32)
        for i in range(3):
            for j in range(3):
                here = pl.ds((i * 3 + j) * channels, channels)
                grad = jnp.dot(xt[...], tap(i, j), preferred_element_type=F32).astype(BF16)
                pair_w[slot, here, :] = grad
                grad = grad.astype(F32)
                own_sq = own_sq + fold(grad * grad)
                if slot:
                    cross = cross + fold(grad * pair_w[0, here, :].astype(F32))
        return own_sq, cross

    stack = []

    def first(k):
        return replica_grad(0, sources[k] * 2 + y)[0]

    def second(k, first_sq):
        source = sources[k]
        for half in range(2):
            copy_of(source * 2 + 1 - y, half, 2, other).wait_recv()
        second_sq, cross = replica_grad(1, source * 2 + 1 - y)
        coefs = coefs_of(first_sq, second_sq, cross)
        lower, upper, target = pair_w.at[0], pair_w.at[1], source
        rest = k + 1
        while True:
            against = merged.at[stack[-1]] if rest % 2 == 0 else None
            coefs = pair_merge(lower, upper, merged.at[target], coefs, against, rows_total, rows)
            if against is None:
                stack.append(target)
                return None
            lower, upper = merged.at[target], against
            target = stack.pop()
            rest //= 2
            if k == chain - 1 and not stack:
                return lower, upper, coefs

    forward(0, (0,))
    z_f = pre_ref[...].astype(F32)
    sig = jax.nn.sigmoid(z_f)
    factors[rep, 1] = (up_ref[...].astype(F32) * sig * (1.0 + z_f * (1.0 - sig))).astype(BF16)
    spread(rep)
    forward(0, (1,))
    load.wait()
    total = jnp.zeros((pixels, channels), F32)
    for i in range(3):
        for j in range(3):
            total = total + lax.dot_general(
                tap(i, j),
                kernel_v[pl.ds((i * 3 + j) * channels, channels), :],
                (((1,), (1,)), ((), ())),
                preferred_element_type=F32,
            )
    igrad[...] = total.astype(BF16)

    @pl.when(pipe == sections - 1)
    def _():
        passed_ref[...] = jnp.zeros_like(passed_ref)

    passing = pltpu.make_async_remote_copy(
        src_ref=igrad,
        dst_ref=passed_ref,
        send_sem=pass_sem.at[0],
        recv_sem=pass_sem.at[1],
        device_id=(jnp.maximum(pipe - 1, 0), rep),
        device_id_type=MESH,
    )

    first_sq = first(0)
    forward(1)

    @pl.when(pipe > 0)
    def _():
        passing.start()

    for k in range(2, chain):
        @pl.when(jnp.abs(sources[k] - z) == 1)
        def _():
            forward(k)

    second(0, first_sq)
    for k in range(1, chain):
        first_sq = first(k)
        if k + 1 < chain:
            @pl.when(jnp.abs(sources[k + 1] - z) != 1)
            def _():
                forward(k + 1)
        result = second(k, first_sq)
    lower, upper, coefs = result

    own_rows = rows_total // replicas
    own = pl.ds(pl.multiple_of(rep * own_rows, own_rows), own_rows)
    final = coefs[0] * lower[own, :].astype(F32) + coefs[1] * upper[own, :].astype(F32)
    combined_ref[...] = final.astype(BF16)

    for k in range(chain):
        source = sources[k]
        block = source * 2 + y
        for half in range(2):
            for way, cond, target in ways(source):
                @pl.when(cond)
                def _():
                    copy_of(block, half, way, target).wait_send()
            copy_of(block, half, 2, other).wait_send()

    @pl.when(pipe > 0)
    def _():
        passing.wait_send()

    @pl.when(pipe < sections - 1)
    def _():
        passing.wait_recv()


def update(combined, master, momentum, passed_in, new_momentum, new_weights, passed_out):
    own_rows, channels = combined.shape
    lanes = momentum.shape[-1]
    groups = channels // lanes
    passed_out[...] = passed_in[...]
    for g in range(groups):
        at = pl.ds(g, own_rows, stride=groups)
        part = combined[:, g * lanes : (g + 1) * lanes].astype(F32)
        moved = 0.9 * momentum[at, :] + 0.0625 * part
        new_momentum[at, :] = moved
        new_weights[at, :] = master[at, :] - 0.02 * moved


def factor_body(sections, replicas, activations, preactivation, upstream, weights, master, momentum):
    tile = activations.shape[3:]
    cols, channels = tile[1], tile[2]
    pixels = tile[0] * cols
    taps_rows = weights.shape[1]
    lanes = 128
    flat = (momentum.shape[2] // lanes, lanes)
    small, big = pl.BlockSpec(memory_space=pltpu.VMEM), pl.BlockSpec(memory_space=pl.ANY)
    passed, combined = pl.pallas_call(
        functools.partial(kernel, sections, replicas, cols),
        out_shape=(
            jax.ShapeDtypeStruct((pixels, channels), BF16),
            jax.ShapeDtypeStruct((taps_rows // replicas, channels), BF16),
        ),
        in_specs=[small, small, small, big],
        out_specs=(small, small),
        scratch_shapes=[
            pltpu.VMEM((replicas, 2, pixels, channels), BF16),
            pltpu.VMEM((3, pixels + 2 * cols, channels), BF16),
            pltpu.VMEM((channels, pixels), BF16),
            pltpu.VMEM((taps_rows, channels), BF16),
            pltpu.VMEM((pixels, channels), BF16),
            pltpu.VMEM((2, taps_rows, channels), BF16),
            pltpu.VMEM((replicas // 2, taps_rows, channels), BF16),
            pltpu.SemaphoreType.DMA((3, replicas, 2)),
            pltpu.SemaphoreType.DMA((replicas, 2)),
            pltpu.SemaphoreType.DMA((2,)),
            pltpu.SemaphoreType.DMA,
        ],
        compiler_params=pltpu.CompilerParams(
            collective_id=0, has_side_effects=True, vmem_limit_bytes=56 * 1024 * 1024
        ),
    )(
        activations.reshape(pixels, channels),
        preactivation.reshape(pixels, channels),
        upstream.reshape(pixels, channels),
        weights[0],
    )
    new_momentum, new_weights, passed = pl.pallas_call(
        update,
        out_shape=(
            jax.ShapeDtypeStruct(flat, F32),
            jax.ShapeDtypeStruct(flat, F32),
            jax.ShapeDtypeStruct((pixels, channels), BF16),
        ),
        in_specs=[small] * 4,
        out_specs=(small,) * 3,
    )(combined, master.reshape(flat), momentum.reshape(flat), passed)
    return (
        passed.reshape(activations.shape),
        new_momentum.reshape(momentum.shape),
        new_weights.reshape(master.shape),
    )


def pick(sections, replicas, *arrays):
    activations, weights, momentum = arrays[0], arrays[3], arrays[5]
    factor = 2 * activations.size
    fits = (
        replicas >= 4
        and replicas & (replicas - 1) == 0
        and activations.shape[2] == 1
        and (replicas - 1) * factor <= 2 * weights.size
        and activations.shape[4] % 16 == 0
        and activations.shape[5] % 128 == 0
        and (weights.shape[1] // replicas) % 16 == 0
        and momentum.shape[2] % 1024 == 0
    )
    return factor_body(sections, replicas, *arrays) if fits else body(*arrays)


def solution(mesh):
    return jax.shard_map(
        functools.partial(pick, mesh.shape["pipe"], mesh.shape["rep"]),
        mesh=mesh,
        in_specs=(
            P("pipe", "rep", None, None, None, None),
            P("pipe", "rep", None, None, None, None),
            P("pipe", "rep", None, None, None, None),
            P("pipe", None, None),
            P("pipe", "rep", None),
            P("pipe", "rep", None),
        ),
        out_specs=(
            P("pipe", "rep", None, None, None, None),
            P("pipe", "rep", None),
            P("pipe", "rep", None),
        ),
        check_vma=False,
    )
```

```python
import functools

import jax
import jax.numpy as jnp
from jax import lax
from jax.experimental import pallas as pl
from jax.experimental.pallas import tpu as pltpu
from jax.sharding import PartitionSpec as P

EPS = 1e-06


def swapped(shard, axis, stride):
    return lax.ppermute(shard, axis, [(i, i ^ 1 << stride) for i in range(lax.axis_size(axis))])


def from_behind(shard, axis, by):
    count = lax.axis_size(axis)
    pairs = [(i, i + by) for i in range(count) if 0 <= i + by < count]
    return lax.ppermute(shard, axis, pairs)


def shifted_patches(tile_data, flipped):
    frames, tile_rows, tile_cols, channels = tile_data.shape
    padded = jnp.pad(tile_data, ((0, 0), (1, 1), (1, 1), (0, 0)))
    if flipped:
        offsets = [(2 - row_off, 2 - col_off) for row_off in range(3) for col_off in range(3)]
    else:
        offsets = [(row_off, col_off) for row_off in range(3) for col_off in range(3)]
    pieces = [
        padded[:, first : first + tile_rows, second : second + tile_cols, :]
        for first, second in offsets
    ]
    return jnp.concatenate(pieces, axis=-1).reshape(frames * tile_rows * tile_cols, 9 * channels)


def local_backward(tile_data, preact_tile, upstream_tile, kernel):
    frames, tile_rows, tile_cols, channels = tile_data.shape
    pre_float = preact_tile.astype(jnp.float32)
    sigmoid_val = jax.nn.sigmoid(pre_float)
    local_grad = (
        upstream_tile.astype(jnp.float32) * sigmoid_val * (1.0 + pre_float * (1.0 - sigmoid_val))
    ).astype(jnp.bfloat16)
    flat_grad = local_grad.reshape(-1, channels)
    patches = shifted_patches(tile_data, False)
    weight_grad = lax.dot_general(
        patches, flat_grad, (((0,), (0,)), ((), ())), preferred_element_type=jnp.float32
    ).astype(jnp.bfloat16)
    grad_patches = shifted_patches(local_grad, True).reshape(-1, 9, channels)
    kernel_taps = kernel.reshape(9, channels, channels)
    summed = lax.dot_general(
        grad_patches, kernel_taps, (((1, 2), (0, 2)), ((), ())), preferred_element_type=jnp.float32
    )
    return (
        weight_grad,
        summed.astype(jnp.bfloat16).reshape(frames, tile_rows, tile_cols, channels),
    )


def group_sum(partials, sum_bits):
    for bit_number in range(sum_bits):
        partials = partials + swapped(partials, "rep", bit_number)
    return partials


def body(activations, preactivation, upstream, weights, master, momentum):
    weight_grad, input_grad = local_backward(
        activations[0, 0], preactivation[0, 0], upstream[0, 0], weights[0]
    )
    passed = from_behind(input_grad, "pipe", -1)
    replicas = lax.axis_size("rep")
    level_count = replicas.bit_length() - 1
    rep_index = lax.axis_index("rep")
    held_rows = weight_grad.reshape(replicas, -1)
    for level_num in range(level_count):
        is_lower = jnp.right_shift(rep_index, level_num) & 1 == 0
        paired = held_rows.reshape(-1, 2, held_rows.shape[1])
        keep_rows = jnp.where(is_lower, paired[:, 0], paired[:, 1])
        give_rows = jnp.where(is_lower, paired[:, 1], paired[:, 0])
        other_rows = swapped(give_rows, "rep", level_num)
        keep_float = keep_rows.astype(jnp.float32)
        other_float = other_rows.astype(jnp.float32)
        keep_sq = jnp.sum(keep_float * keep_float)
        other_sq = jnp.sum(other_float * other_float)
        partials = jnp.stack(
            [
                jnp.where(is_lower, keep_sq, other_sq),
                jnp.where(is_lower, other_sq, keep_sq),
                jnp.sum(keep_float * other_float),
            ]
        )
        sum_bits = level_num + 1
        partials = group_sum(partials, sum_bits)
        lower_coef = 1.0 - partials[2] / (2.0 * partials[0] + EPS)
        upper_coef = 1.0 - partials[2] / (2.0 * partials[1] + EPS)
        keep_coef = jnp.where(is_lower, lower_coef, upper_coef)
        other_coef = jnp.where(is_lower, upper_coef, lower_coef)
        merged = keep_coef * keep_rows.astype(jnp.float32) + other_coef * other_rows.astype(
            jnp.float32
        )
        held_rows = merged.astype(jnp.bfloat16)
    combined = held_rows.astype(jnp.float32).reshape(momentum.shape)
    new_momentum = 0.9 * momentum + 0.0625 * combined
    new_weights = master - 0.02 * new_momentum
    return (passed[None, None], new_momentum, new_weights)

MESH = pl.DeviceIdType.MESH
F32 = jnp.float32
BF16 = jnp.bfloat16


def chunk_rows(channels):
    return next(rows for rows in (32, 16) if channels % rows == 0)


def fold(product):
    return jnp.sum(product.reshape(-1, 8, product.shape[-1]), axis=0)


def coefs_of(lower_sq, upper_sq, cross):
    aa, bb, ab = jnp.sum(lower_sq), jnp.sum(upper_sq), jnp.sum(cross)
    return 1.0 - ab / (2.0 * aa + EPS), 1.0 - ab / (2.0 * bb + EPS)


def pair_merge(lower, upper, target, coefs, against, rows_total, rows):
    channels = lower.shape[-1]

    def step(i, sums):
        here = pl.ds(pl.multiple_of(i * rows, rows), rows)
        a, b = lower[here, :].astype(F32), upper[here, :].astype(F32)
        new = (coefs[0] * a + coefs[1] * b).astype(BF16)
        target[here, :] = new
        if against is None:
            return sums
        new, next_one = new.astype(F32), against[here, :].astype(F32)
        return (
            sums[0] + fold(new * new),
            sums[1] + fold(next_one * next_one),
            sums[2] + fold(new * next_one),
        )

    zero = jnp.zeros((8, channels), F32)
    init = () if against is None else (zero, zero, zero)
    count = rows_total // rows
    sums = lax.fori_loop(0, count, step, init, unroll=next(n for n in (3, 2, 1) if count % n == 0))
    return None if against is None else coefs_of(*sums)


def kernel(
    sections, replicas, cols,
    act_ref, pre_ref, up_ref, weights_hbm,
    passed_ref, combined_ref,
    factors, shifted, xt, kernel_v, igrad, pair_w, merged,
    send_sem, recv_sem, pass_sem, load_sem,
):
    pixels, channels = act_ref.shape
    rows_total = kernel_v.shape[0]
    rows = chunk_rows(channels)
    pipe, rep = lax.axis_index("pipe"), lax.axis_index("rep")
    chain = replicas // 2
    z, y = rep // 2, rep % 2
    other = z * 2 + 1 - y

    barrier = pltpu.get_barrier_semaphore()

    def greet(cond, device):
        @pl.when(cond)
        def _():
            pl.semaphore_signal(barrier, inc=1, device_id=device, device_id_type=MESH)

    pl.semaphore_signal(barrier, inc=1, device_id=(pipe, other), device_id_type=MESH)
    greet(z > 0, (pipe, rep - 2))
    greet(z < chain - 1, (pipe, rep + 2))
    greet(pipe < sections - 1, (pipe + 1, rep))

    load = pltpu.make_async_copy(weights_hbm, kernel_v, load_sem)
    load.start()
    factors[rep, 0] = act_ref[...]

    edge = jnp.zeros((cols, channels), BF16)
    for j in range(3):
        shifted[j, pl.ds(0, cols), :] = edge
        shifted[j, pl.ds(cols + pixels, cols), :] = edge

    def spread(block):
        grad = factors[block, 1].astype(F32)
        column = lax.broadcasted_iota(jnp.int32, (pixels, channels), 0) % cols
        here = pl.ds(cols, pixels)
        shifted[0, here, :] = jnp.where(
            column < cols - 1, pltpu.roll(grad, pixels - 1, 0), 0.0
        ).astype(BF16)
        shifted[1, here, :] = factors[block, 1]
        shifted[2, here, :] = jnp.where(column > 0, pltpu.roll(grad, 1, 0), 0.0).astype(BF16)

    def tap(i, j):
        return shifted[j, pl.ds((2 - i) * cols, pixels), :]

    met = 1 + (z > 0).astype(jnp.int32) + (z < chain - 1).astype(jnp.int32)
    pl.semaphore_wait(barrier, met + (pipe > 0).astype(jnp.int32))

    def copy_of(block, half, way, target):
        return pltpu.make_async_remote_copy(
            src_ref=factors.at[block, half],
            dst_ref=factors.at[block, half],
            send_sem=send_sem.at[way, block, half],
            recv_sem=recv_sem.at[block, half],
            device_id=(pipe, target),
            device_id_type=MESH,
        )

    def ways(source):
        return (
            (0, (source <= z) & (z < chain - 1), jnp.minimum(rep + 2, replicas - 1)),
            (1, (source >= z) & (z > 0), jnp.maximum(rep - 2, 0)),
        )

    def order(k):
        if k == 0:
            return z
        size = 1 << (k.bit_length() - 1)
        step, group = k - size, z // size
        return jnp.where(
            group % 2 == 0, (group + 1) * size + step, group * size - 1 - step
        )

    sources = [order(k) for k in range(chain)]

    def forward(k, halves=(0, 1)):
        source = sources[k]
        block = source * 2 + y
        for half in halves:
            if k:
                copy_of(block, half, 2, other).wait_recv()
            for way, cond, target in ways(source):
                @pl.when(cond)
                def _():
                    copy_of(block, half, way, target).start()
            copy_of(block, half, 2, other).start()

    def replica_grad(slot, block):
        spread(block)
        xt[...] = factors[block, 0].T
        own_sq = jnp.zeros((8, channels), F32)
        cross = jnp.zeros((8, channels), F32)
        for i in range(3):
            for j in range(3):
                here = pl.ds((i * 3 + j) * channels, channels)
                grad = jnp.dot(xt[...], tap(i, j), preferred_element_type=F32).astype(BF16)
                pair_w[slot, here, :] = grad
                grad = grad.astype(F32)
                own_sq = own_sq + fold(grad * grad)
                if slot:
                    cross = cross + fold(grad * pair_w[0, here, :].astype(F32))
        return own_sq, cross

    stack = []

    def first(k):
        return replica_grad(0, sources[k] * 2 + y)[0]

    def second(k, first_sq):
        source = sources[k]
        for half in range(2):
            copy_of(source * 2 + 1 - y, half, 2, other).wait_recv()
        second_sq, cross = replica_grad(1, source * 2 + 1 - y)
        coefs = coefs_of(first_sq, second_sq, cross)
        lower, upper, target = pair_w.at[0], pair_w.at[1], source
        rest = k + 1
        while True:
            against = merged.at[stack[-1]] if rest % 2 == 0 else None
            coefs = pair_merge(lower, upper, merged.at[target], coefs, against, rows_total, rows)
            if against is None:
                stack.append(target)
                return None
            lower, upper = merged.at[target], against
            target = stack.pop()
            rest //= 2
            if k == chain - 1 and not stack:
                return lower, upper, coefs

    forward(0, (0,))
    z_f = pre_ref[...].astype(F32)
    sig = jax.nn.sigmoid(z_f)
    factors[rep, 1] = (up_ref[...].astype(F32) * sig * (1.0 + z_f * (1.0 - sig))).astype(BF16)
    spread(rep)
    forward(0, (1,))
    load.wait()
    total = jnp.zeros((pixels, channels), F32)
    for i in range(3):
        for j in range(3):
            total = total + lax.dot_general(
                tap(i, j),
                kernel_v[pl.ds((i * 3 + j) * channels, channels), :],
                (((1,), (1,)), ((), ())),
                preferred_element_type=F32,
            )
    igrad[...] = total.astype(BF16)

    @pl.when(pipe == sections - 1)
    def _():
        passed_ref[...] = jnp.zeros_like(passed_ref)

    passing = pltpu.make_async_remote_copy(
        src_ref=igrad,
        dst_ref=passed_ref,
        send_sem=pass_sem.at[0],
        recv_sem=pass_sem.at[1],
        device_id=(jnp.maximum(pipe - 1, 0), rep),
        device_id_type=MESH,
    )

    first_sq = first(0)
    forward(1)

    @pl.when(pipe > 0)
    def _():
        passing.start()

    for k in range(2, chain):
        @pl.when(jnp.abs(sources[k] - z) == 1)
        def _():
            forward(k)

    second(0, first_sq)
    for k in range(1, chain):
        first_sq = first(k)
        if k + 1 < chain:
            @pl.when(jnp.abs(sources[k + 1] - z) != 1)
            def _():
                forward(k + 1)
        result = second(k, first_sq)
    lower, upper, coefs = result

    own_rows = rows_total // replicas
    own = pl.ds(pl.multiple_of(rep * own_rows, own_rows), own_rows)
    final = coefs[0] * lower[own, :].astype(F32) + coefs[1] * upper[own, :].astype(F32)
    combined_ref[...] = final.astype(BF16)

    for k in range(chain):
        source = sources[k]
        block = source * 2 + y
        for half in range(2):
            for way, cond, target in ways(source):
                @pl.when(cond)
                def _():
                    copy_of(block, half, way, target).wait_send()
            copy_of(block, half, 2, other).wait_send()

    @pl.when(pipe > 0)
    def _():
        passing.wait_send()

    @pl.when(pipe < sections - 1)
    def _():
        passing.wait_recv()


def update(combined, master, momentum, passed_in, new_momentum, new_weights, passed_out):
    own_rows, channels = combined.shape
    lanes = momentum.shape[-1]
    groups = channels // lanes
    passed_out[...] = passed_in[...]
    for g in range(groups):
        at = pl.ds(g, own_rows, stride=groups)
        part = combined[:, g * lanes : (g + 1) * lanes].astype(F32)
        moved = 0.9 * momentum[at, :] + 0.0625 * part
        new_momentum[at, :] = moved
        new_weights[at, :] = master[at, :] - 0.02 * moved


def factor_body(sections, replicas, activations, preactivation, upstream, weights, master, momentum):
    tile = activations.shape[3:]
    cols, channels = tile[1], tile[2]
    pixels = tile[0] * cols
    taps_rows = weights.shape[1]
    lanes = 128
    flat = (momentum.shape[2] // lanes, lanes)
    small, big = pl.BlockSpec(memory_space=pltpu.VMEM), pl.BlockSpec(memory_space=pl.ANY)
    passed, combined = pl.pallas_call(
        functools.partial(kernel, sections, replicas, cols),
        out_shape=(
            jax.ShapeDtypeStruct((pixels, channels), BF16),
            jax.ShapeDtypeStruct((taps_rows // replicas, channels), BF16),
        ),
        in_specs=[small, small, small, big],
        out_specs=(small, small),
        scratch_shapes=[
            pltpu.VMEM((replicas, 2, pixels, channels), BF16),
            pltpu.VMEM((3, pixels + 2 * cols, channels), BF16),
            pltpu.VMEM((channels, pixels), BF16),
            pltpu.VMEM((taps_rows, channels), BF16),
            pltpu.VMEM((pixels, channels), BF16),
            pltpu.VMEM((2, taps_rows, channels), BF16),
            pltpu.VMEM((replicas // 2, taps_rows, channels), BF16),
            pltpu.SemaphoreType.DMA((3, replicas, 2)),
            pltpu.SemaphoreType.DMA((replicas, 2)),
            pltpu.SemaphoreType.DMA((2,)),
            pltpu.SemaphoreType.DMA,
        ],
        compiler_params=pltpu.CompilerParams(
            collective_id=0, has_side_effects=True, vmem_limit_bytes=56 * 1024 * 1024
        ),
    )(
        activations.reshape(pixels, channels),
        preactivation.reshape(pixels, channels),
        upstream.reshape(pixels, channels),
        weights[0],
    )
    new_momentum, new_weights, passed = pl.pallas_call(
        update,
        out_shape=(
            jax.ShapeDtypeStruct(flat, F32),
            jax.ShapeDtypeStruct(flat, F32),
            jax.ShapeDtypeStruct((pixels, channels), BF16),
        ),
        in_specs=[small] * 4,
        out_specs=(small,) * 3,
    )(combined, master.reshape(flat), momentum.reshape(flat), passed)
    return (
        passed.reshape(activations.shape),
        new_momentum.reshape(momentum.shape),
        new_weights.reshape(master.shape),
    )


def pick(sections, replicas, *arrays):
    activations, weights, momentum = arrays[0], arrays[3], arrays[5]
    factor = 2 * activations.size
    fits = (
        replicas >= 4
        and replicas & (replicas - 1) == 0
        and activations.shape[2] == 1
        and (replicas - 1) * factor <= 2 * weights.size
        and activations.shape[4] % 16 == 0
        and activations.shape[5] % 128 == 0
        and (weights.shape[1] // replicas) % 16 == 0
        and momentum.shape[2] % 1024 == 0
    )
    return factor_body(sections, replicas, *arrays) if fits else body(*arrays)


def solution(mesh):
    return jax.shard_map(
        functools.partial(pick, mesh.shape["pipe"], mesh.shape["rep"]),
        mesh=mesh,
        in_specs=(
            P("pipe", "rep", None, None, None, None),
            P("pipe", "rep", None, None, None, None),
            P("pipe", "rep", None, None, None, None),
            P("pipe", None, None),
            P("pipe", "rep", None),
            P("pipe", "rep", None),
        ),
        out_specs=(
            P("pipe", "rep", None, None, None, None),
            P("pipe", "rep", None),
            P("pipe", "rep", None),
        ),
        check_vma=False,
    )
```
